32 devices in a mesh: clip: 4 (over z), head: 8 (over y, x, core).
Axes of the slice: x: 2, y: 2, z: 4, core: 2. Of those that a mesh axis runs over, the one named last changes fastest.
Arguments:
- tokens: bfloat16 [10240, 2048], P('clip'), may hold values from -6 to 6
- frame_count: int32 [4], P('clip'), may hold values from 3 to 4
- norm1_gain: float32 [2048], replicated, may hold values from 0.1 to 1.9
- w_query: bfloat16 [2048, 2048], P(None, 'head'), may hold values from -0.125 to 0.125
- w_key: bfloat16 [2048, 2048], P(None, 'head'), may hold values from -0.125 to 0.125
- w_value: bfloat16 [2048, 2048], P(None, 'head'), may hold values from -0.125 to 0.125
- w_out: bfloat16 [2048, 2048], P('head'), may hold values from -2 to 2
- norm2_gain: float32 [2048], replicated, may hold values from 0.1 to 1.9
- w_up: bfloat16 [2048, 8192], P(None, 'head'), may hold values from -0.125 to 0.125
- w_down: bfloat16 [8192, 2048], P('head'), may hold values from -0.0625 to 0.0625
- out_grad: bfloat16 [10240, 2048], P('clip'), may hold values from -6 to 6
Outputs:
- output: bfloat16 [10240, 2048], P('clip')
- in_grad: bfloat16 [10240, 2048], P('clip')
- grad_norm1: float32 [2048], P('clip')
- grad_w_query: float32 [2048, 2048], P('clip', 'head')
- grad_w_key: float32 [2048, 2048], P('clip', 'head')
- grad_w_value: float32 [2048, 2048], P('clip', 'head')
- grad_w_out: float32 [2048, 2048], P('head', 'clip')
- grad_norm2: float32 [2048], P('clip')
- grad_w_up: float32 [2048, 8192], P('clip', 'head')
- grad_w_down: float32 [8192, 2048], P('head', 'clip')
The draws below stay inside these ranges and needn't reach their ends.
Inputs may be any that keep to these rules, and one draw needn't show every extreme that they name: frame_count gives each clip's real frames; the rows of slots from that count on are padding.
All inputs are finite; a program needn't handle non-finite values.
Results may differ from the reference program's by a relative error of at most 0.023.
Values may be sent and summed in bfloat16 or wider, within the bound.
No kernel may reach another device: no remote copies, remote signals or barrier semaphores. Data moves between devices by JAX's collectives and lax.ppermute only.
A program may use at most 256 MiB of HBM per device.

```python
import math
import jax
import jax.numpy as jnp
from jax import lax

D = 2048
HEADS = 16
HEAD_DIM = 128
FF = 8192
FRAME = 640
SLOTS = 4
BLOCK = 512
CLIP_LEN = 2560
CLIPS = 4
TOKENS = 10240
HEADS_DEV = 2
FF_DEV = 1024
N_HEAD = 8


def plant(entries, own_key, low, top_value):
    extent = entries.shape
    place = [jax.random.randint(jax.random.fold_in(own_key, axis), (), 0, extent[axis]) for axis in range(len(extent))]
    entries = entries.at[tuple(place)].set(low)
    longest = extent.index(max(extent))
    place[longest] = (place[longest] + 1) % extent[longest]
    return entries.at[tuple(place)].set(top_value)


def levels(stream_key, dims, split, least, top_value):
    def one(position, blocks):
        steps = jax.random.uniform(jax.random.fold_in(jax.random.fold_in(stream_key, 6), position), (blocks,), jnp.float32, least / len(split), top_value / len(split))
        return jnp.repeat(jnp.exp(steps), dims[position] // blocks).reshape((-1,) + (1,) * (len(dims) - position - 1))

    level = one(*split[0])
    for cut in split[1:]:
        level = level * one(*cut)
    return level


def scatter_about(stream_key, shape, spread, most, cuts=(), kind=jnp.bfloat16):
    entries = spread * jax.random.normal(stream_key, shape, jnp.float32)
    if cuts:
        entries = entries * levels(stream_key, shape, cuts, -0.22, 0.18)
    return jnp.clip(entries, -most, most).astype(kind)


def setup_inputs(seed: int = 0) -> dict:
    arg_keys = jax.random.split(jax.random.key(seed), 12)
    tokens = scatter_about(arg_keys[0], (TOKENS, D), 1.0, 6.0, ((0, 4),))
    frame_count = plant(jax.random.randint(arg_keys[1], (CLIPS,), SLOTS - 1, SLOTS + 1), jax.random.fold_in(arg_keys[1], 1), SLOTS - 1, SLOTS).astype(jnp.int32)
    norm1_gain = jnp.clip(1.0 + 0.18 * jax.random.normal(arg_keys[2], (D,), jnp.float32), 0.1, 1.9)
    w_query = scatter_about(arg_keys[3], (D, HEADS * HEAD_DIM), D ** -0.5, 0.125, ((1, 8),))
    w_key = scatter_about(arg_keys[4], (D, HEADS * HEAD_DIM), D ** -0.5, 0.125, ((1, 8),))
    w_value = scatter_about(arg_keys[5], (D, HEADS * HEAD_DIM), D ** -0.5, 0.125, ((1, 8),))
    w_out = scatter_about(arg_keys[6], (HEADS * HEAD_DIM, D), (max(D // 256, 2)) ** -0.5, 2.0, ((0, 8),))
    norm2_gain = jnp.clip(1.0 + 0.18 * jax.random.normal(arg_keys[7], (D,), jnp.float32), 0.1, 1.9)
    w_up = scatter_about(arg_keys[8], (D, FF), D ** -0.5, 0.125, ((1, 8),))
    w_down = scatter_about(arg_keys[9], (FF, D), FF ** -0.5, 0.0625, ((0, 8),))
    out_grad = scatter_about(arg_keys[10], (TOKENS, D), 1.0, 6.0, ((0, 4),))
    return dict(tokens=tokens, frame_count=frame_count, norm1_gain=norm1_gain, w_query=w_query, w_key=w_key, w_value=w_value, w_out=w_out, norm2_gain=norm2_gain, w_up=w_up, w_down=w_down, out_grad=out_grad)


@jax.custom_vjp
def low(v):
    return lax.optimization_barrier(v.astype(jnp.bfloat16)).astype(jnp.float32)

@jax.custom_vjp
def low_back(v):
    return v

def low_keep(v):
    return (low(v), None)

def low_pass(kept, grad):
    return (grad,)

def back_keep(v):
    return (v, None)

def back_low(kept, grad):
    return (low(grad),)
low.defvjp(low_keep, low_pass)
low_back.defvjp(back_keep, back_low)

def layer_norm(values, gain):
    row_mean = lax.optimization_barrier(jnp.mean(values, axis=-1, keepdims=True))
    centered = values - row_mean
    variance = lax.optimization_barrier(jnp.mean(centered * centered, axis=-1, keepdims=True))
    return centered * lax.rsqrt(variance + 1e-05) * gain

def rotary_tables(length):
    positions = jnp.arange(length, dtype=jnp.int32).astype(jnp.float32)
    half_dim = HEAD_DIM // 2
    lane_index = (jnp.arange(HEAD_DIM, dtype=jnp.int32) % half_dim).astype(jnp.float32)
    frequency = jnp.exp(lane_index * (-2.0 * math.log(10000.0) / HEAD_DIM))
    angles = positions[:, None] * frequency[None, :]
    return (jnp.cos(angles), jnp.sin(angles))

def rotate(values, cos_table, sin_table):
    half_dim = HEAD_DIM // 2
    turned = jnp.concatenate([-values[..., half_dim:], values[..., :half_dim]], axis=-1)
    return values * cos_table[:, None, :] + turned * sin_table[:, None, :]

def exact_dot(left, right):
    return jnp.dot(left, right, precision=lax.Precision.HIGHEST)

def attention_heads(query, key_rot, values_low, row_live):
    score_scale = 1.0 / math.sqrt(HEAD_DIM)
    key_index = jnp.arange(CLIP_LEN, dtype=jnp.int32)
    key_ok = row_live > 0

    def block_fn(start):
        q_block = lax.dynamic_slice_in_dim(query, start, BLOCK, 0)
        q_pos = start + jnp.arange(BLOCK, dtype=jnp.int32)
        raw_scores = jnp.einsum('thd,shd->hts', q_block, key_rot, precision=lax.Precision.HIGHEST)
        scores = low_back(raw_scores * score_scale)
        allowed = (key_index[None, :] <= q_pos[:, None]) & key_ok[None, :]
        scores = jnp.where(allowed[None], scores, -1e+30)
        log_total = jax.nn.logsumexp(scores, axis=-1, keepdims=True)
        probabilities = jnp.exp(scores - log_total)
        return jnp.einsum('hts,shd->thd', low(probabilities), values_low, precision=lax.Precision.HIGHEST)
    starts = jnp.arange(CLIP_LEN // BLOCK, dtype=jnp.int32) * BLOCK
    blocks = lax.map(jax.checkpoint(block_fn), starts)
    return blocks.reshape(CLIP_LEN, HEADS_DEV * HEAD_DIM)

def forward(inputs, norm1_gain, w_query, w_key, w_value, w_out, norm2_gain, w_up, w_down, row_live, cos_table, sin_table):
    group_width = HEADS_DEV * HEAD_DIM
    norm1 = low(layer_norm(inputs, norm1_gain))
    attn_total = jnp.zeros_like(inputs)
    for group in range(N_HEAD):
        columns = slice(group * group_width, (group + 1) * group_width)
        group_norm = low_back(norm1)
        query_lin = low_back(exact_dot(group_norm, w_query[:, columns])).reshape(CLIP_LEN, HEADS_DEV, HEAD_DIM)
        key_lin = low_back(exact_dot(group_norm, w_key[:, columns])).reshape(CLIP_LEN, HEADS_DEV, HEAD_DIM)
        query = low(rotate(query_lin, cos_table, sin_table))
        key_rot = low(rotate(key_lin, cos_table, sin_table))
        values_low = low(low_back(exact_dot(group_norm, w_value[:, columns]))).reshape(CLIP_LEN, HEADS_DEV, HEAD_DIM)
        mixed_heads = low(low_back(attention_heads(query, key_rot, values_low, row_live)))
        attn_total = attn_total + low(exact_dot(mixed_heads, w_out[columns, :]))
    hidden_res = inputs + row_live[:, None] * low_back(attn_total)
    norm2 = low(layer_norm(hidden_res, norm2_gain))
    mlp_total = jnp.zeros_like(inputs)
    for group in range(N_HEAD):
        columns = slice(group * FF_DEV, (group + 1) * FF_DEV)
        group_norm = low_back(norm2)
        up_proj = low_back(exact_dot(group_norm, w_up[:, columns]))
        activated = low(jax.nn.gelu(up_proj, approximate=True))
        mlp_total = mlp_total + low(exact_dot(activated, w_down[columns, :]))
    return hidden_res + row_live[:, None] * low_back(mlp_total)

def reference(tokens, frame_count, norm1_gain, w_query, w_key, w_value, w_out, norm2_gain, w_up, w_down, out_grad):
    params = (norm1_gain.astype(jnp.float32), w_query.astype(jnp.float32), w_key.astype(jnp.float32), w_value.astype(jnp.float32), w_out.astype(jnp.float32), norm2_gain.astype(jnp.float32), w_up.astype(jnp.float32), w_down.astype(jnp.float32))
    inputs_all = tokens.astype(jnp.float32).reshape(CLIPS, CLIP_LEN, D)
    grads_all = out_grad.astype(jnp.float32).reshape(CLIPS, CLIP_LEN, D)
    cos_table, sin_table = rotary_tables(CLIP_LEN)

    def one_clip(totals, items):
        inputs, cotangent, frame_total = items
        slot_index = jnp.arange(CLIP_LEN, dtype=jnp.int32) // FRAME
        row_live = (slot_index < frame_total).astype(jnp.float32)

        def layer_fn(inputs_in, *weights):
            return forward(inputs_in, *weights, row_live, cos_table, sin_table)
        result, pullback = jax.vjp(layer_fn, inputs, *params)
        grads = pullback(cotangent)
        totals = tuple((total + grad for total, grad in zip(totals, grads[1:])))
        return (totals, (result.astype(jnp.bfloat16), grads[0].astype(jnp.bfloat16)))
    zero_grads = tuple((jnp.zeros_like(param) for param in params))
    totals, (outputs, in_grads) = lax.scan(one_clip, zero_grads, (inputs_all, grads_all, frame_count))
    return (outputs.reshape(TOKENS, D), in_grads.reshape(TOKENS, D), totals[0], totals[1], totals[2], totals[3], totals[4], totals[5], totals[6], totals[7])
```

```python
from functools import partial
import math

import jax
import jax.numpy as jnp
from jax import lax
from jax.experimental import pallas as pl
from jax.experimental.pallas import tpu as pltpu
from jax.sharding import PartitionSpec as P

HEAD_DIM = 128
FRAME = 640
F32 = jnp.float32
BF16 = jnp.bfloat16
SCALE = 1.0 / math.sqrt(HEAD_DIM)
SCALE2 = SCALE / math.log(2.0)
GELU_C = math.sqrt(2.0 / math.pi)
MIB = 1 << 20


def dot_nn(a, b):
    return lax.dot_general(a, b, (((1,), (0,)), ((), ())), preferred_element_type=F32)


def dot_nt(a, b):
    return lax.dot_general(a, b, (((1,), (1,)), ((), ())), preferred_element_type=F32)


def dot_tn(a, b):
    return lax.dot_general(a, b, (((0,), (0,)), ((), ())), preferred_element_type=F32)


def params(vmem_mib=None):
    return pltpu.CompilerParams(
        vmem_limit_bytes=None if vmem_mib is None else vmem_mib * MIB
    )


def cost(flops, nbytes, exps=0):
    return pl.CostEstimate(flops=int(flops), bytes_accessed=int(nbytes), transcendentals=int(exps))


def whole(shape):
    zeros = (0,) * len(shape)
    return pl.BlockSpec(shape, lambda *_: zeros)


def once(shape):
    zeros = (0,) * len(shape)
    return pl.BlockSpec(shape, lambda *_: zeros, pipeline_mode=pl.Buffered(1))


def flip(values):
    return jnp.concatenate(
        [values[:, HEAD_DIM // 2 :], values[:, : HEAD_DIM // 2]], axis=1
    )


def normalize(x):
    mean = jnp.mean(x, axis=-1, keepdims=True)
    centered = x - mean
    inv = lax.rsqrt(jnp.mean(centered * centered, axis=-1, keepdims=True) + 1e-05)
    return centered * inv, inv


def qkv_kernel(
    tok, gain, wq, wk, wv, cj, sj, ci, si, norm_o, q_o, k_o, v_o, cos_o, sin_o
):
    step = pl.program_id(0)
    xhat, _ = normalize(tok[...].astype(F32))
    norm = (xhat * gain[...]).astype(BF16)
    norm_o[...] = norm
    ca, sa = ci[pl.ds(step, 1), :], si[pl.ds(step, 1), :]
    cb, sb = cj[...], sj[...]
    cos = ca * cb - sa * sb
    sin = sa * cb + ca * sb
    lane = lax.broadcasted_iota(jnp.int32, sin.shape, 1)
    sin = jnp.where(lane < HEAD_DIM // 2, -sin, sin)
    cos_o[...] = cos
    sin_o[...] = sin
    for w, o in ((wq, q_o), (wk, k_o)):
        lin = dot_nn(norm, w[...])
        for start in range(0, lin.shape[1], HEAD_DIM):
            part = lin[:, start : start + HEAD_DIM]
            o[:, start : start + HEAD_DIM] = (part * cos + flip(part) * sin).astype(BF16)
    v_o[...] = dot_nn(norm, wv[...]).astype(BF16)


def project(tokens, gain, wq, wk, wv, blocks):
    length, width = tokens.shape
    cols = wq.shape[1]
    rows = length // blocks
    half = HEAD_DIM // 2
    lane = (jnp.arange(HEAD_DIM, dtype=jnp.int32) % half).astype(F32)
    freq = jnp.exp(lane * (-2.0 * math.log(10000.0) / HEAD_DIM))
    fine = jnp.arange(rows, dtype=F32)[:, None] * freq[None, :]
    coarse = (jnp.arange(blocks, dtype=F32) * rows)[:, None] * freq[None, :]
    row = lambda n: pl.BlockSpec((rows, n), lambda i: (i, 0))
    return pl.pallas_call(
        qkv_kernel,
        grid=(blocks,),
        in_specs=[
            row(width),
            whole((1, width)),
            once((width, cols)),
            once((width, cols)),
            once((width, cols)),
            whole((rows, HEAD_DIM)),
            whole((rows, HEAD_DIM)),
            whole((blocks, HEAD_DIM)),
            whole((blocks, HEAD_DIM)),
        ],
        out_specs=[row(width), row(cols), row(cols), row(cols), row(HEAD_DIM), row(HEAD_DIM)],
        out_shape=[
            jax.ShapeDtypeStruct((length, width), BF16),
            jax.ShapeDtypeStruct((length, cols), BF16),
            jax.ShapeDtypeStruct((length, cols), BF16),
            jax.ShapeDtypeStruct((length, cols), BF16),
            jax.ShapeDtypeStruct((length, HEAD_DIM), F32),
            jax.ShapeDtypeStruct((length, HEAD_DIM), F32),
        ],
        compiler_params=params(32),
        cost_estimate=cost(6 * length * width * cols, 4 * length * width),
        name="qkv",
    )(tokens, gain[None, :], wq, wk, wv, jnp.cos(fine), jnp.sin(fine), jnp.cos(coarse), jnp.sin(coarse))


def attend_kernel(rows, chunk, ids, q_ref, k_ref, v_ref, mixed_o, log_o):
    step = pl.program_id(0)
    heads = q_ref.shape[1] // HEAD_DIM
    base = step * rows
    full = base // chunk

    def block(b, carry, masked):
        start = pl.multiple_of(b * chunk, chunk)
        out = []
        for h in range(heads):
            cols = slice(h * HEAD_DIM, (h + 1) * HEAD_DIM)
            peak, total, acc = carry[h]
            s = dot_nt(q_ref[:, cols], k_ref[pl.ds(start, chunk), cols]) * SCALE2
            if masked:
                t_pos = base + lax.broadcasted_iota(jnp.int32, s.shape, 0)
                s_pos = start + lax.broadcasted_iota(jnp.int32, s.shape, 1)
                s = jnp.where(s_pos <= t_pos, s, -1e30)
            top = jnp.maximum(peak, jnp.max(s, axis=1, keepdims=True))
            p = jnp.exp2(s - top)
            old = jnp.exp2(peak - top)
            total = total * old + jnp.sum(p, axis=1, keepdims=True)
            acc = acc * old + dot_nn(p.astype(BF16), v_ref[pl.ds(start, chunk), cols])
            out.append((top, total, acc))
        return tuple(out)

    init = tuple(
        (
            jnp.full((rows, 1), -1e30, F32),
            jnp.zeros((rows, 1), F32),
            jnp.zeros((rows, HEAD_DIM), F32),
        )
        for _ in range(heads)
    )
    carry = lax.fori_loop(0, full, lambda b, c: block(b, c, False), init)
    carry = block(full, carry, True)
    for h in range(heads):
        peak, total, acc = carry[h]
        mixed_o[0, :, h * HEAD_DIM : (h + 1) * HEAD_DIM] = (acc / total).astype(BF16)
        logs = jnp.broadcast_to(peak + jnp.log2(total), (rows, HEAD_DIM))
        log_o[0, h : h + 1, :] = jnp.transpose(logs)[0:1, :]


def attend(ids, q, k, v, blocks):
    length, cols = q.shape
    rows = length // blocks
    heads = cols // HEAD_DIM
    return pl.pallas_call(
        partial(attend_kernel, rows, FRAME),
        grid_spec=pltpu.PrefetchScalarGridSpec(
            num_scalar_prefetch=1,
            grid=(blocks,),
            in_specs=[
                pl.BlockSpec((rows, cols), lambda i, ids: (i, 0)),
                whole((length, cols)),
                whole((length, cols)),
            ],
            out_specs=[
                pl.BlockSpec((1, rows, cols), lambda i, ids: (i ^ ids[0], 0, 0)),
                pl.BlockSpec((1, heads, rows), lambda i, ids: (i, 0, 0)),
            ],
        ),
        out_shape=[
            jax.ShapeDtypeStruct((blocks, rows, cols), BF16),
            jax.ShapeDtypeStruct((blocks, heads, rows), F32),
        ],
        compiler_params=params(40),
        cost_estimate=cost(2.5 * length * length * cols, 8 * length * cols, length * length),
        name="attend",
    )(ids, q, k, v)


def merge_kernel(n, rows, ids, *refs):
    mixed, weights = refs[:n], refs[n : 2 * n]
    tok, gain, res_o, norm_o = refs[2 * n :]
    total = dot_nn(mixed[0][...], weights[0][...])
    for m, w in zip(mixed[1:], weights[1:]):
        total = total + dot_nn(m[...], w[...])
    t_pos = ids[0] * rows + lax.broadcasted_iota(jnp.int32, (rows, 1), 0)
    live = (t_pos < ids[1] * FRAME).astype(F32)
    res = tok[...].astype(F32) + live * total
    res_o[...] = res
    xhat, _ = normalize(res)
    norm_o[...] = (xhat * gain[...]).astype(BF16)


def merge(ids, mixed, weights, tokens, gain):
    n = len(mixed)
    rows, cols = mixed[0].shape
    width = tokens.shape[1]
    return pl.pallas_call(
        partial(merge_kernel, n, rows),
        grid_spec=pltpu.PrefetchScalarGridSpec(
            num_scalar_prefetch=1,
            grid=(1,),
            in_specs=[once((rows, cols))] * n
            + [once((cols, width))] * n
            + [pl.BlockSpec((rows, width), lambda i, ids: (ids[0], 0)), once((1, width))],
            out_specs=[whole((rows, width)), whole((rows, width))],
        ),
        out_shape=[
            jax.ShapeDtypeStruct((rows, width), F32),
            jax.ShapeDtypeStruct((rows, width), BF16),
        ],
        compiler_params=params(48),
        cost_estimate=cost(2 * rows * width * cols * n, 2 * n * cols * width + 12 * rows * width),
        name="merge",
    )(ids, *mixed, *weights, tokens, gain[None, :])


def mlp_kernel(rows, pair, first, ids, *refs):
    n2e, n2o, og, w_up, w_down = refs[:5]
    rest = refs[5:] if first else refs[9:]
    act_o, dup_o, n2_o, dm_o, dne_o, dno_o, mle_o, mlo_o = rest
    step = pl.program_id(0)

    def half(n2, dn_o, ml_o):
        norm = n2[...]
        n2_o[0] = norm
        block = (2 * pair + step) ^ ids[0]
        t_pos = block * rows + lax.broadcasted_iota(jnp.int32, (rows, 1), 0)
        grad = jnp.where(t_pos < ids[1] * FRAME, og[...], jnp.zeros_like(og[...]))
        dm_o[0] = grad
        up = dot_nn(norm, w_up[...])
        d_act = dot_nt(grad, w_down[...])
        square = up * up
        th = jnp.tanh(GELU_C * up * (1.0 + 0.044715 * square))
        gate = 0.5 * (1.0 + th)
        act = (up * gate).astype(BF16)
        slope = gate + 0.5 * up * (1.0 - th * th) * (GELU_C * (1.0 + 0.134145 * square))
        d_up = (d_act * slope).astype(BF16)
        act_o[0] = act
        dup_o[0] = d_up
        dn_o[...] = dot_nt(d_up, w_up[...]).astype(BF16)
        ml_o[...] = dot_nn(act, w_down[...]).astype(BF16)

    @pl.when(step == 0)
    def _():
        half(n2e, dne_o, mle_o)

    @pl.when(step == 1)
    def _():
        half(n2o, dno_o, mlo_o)


def mlp(ids, pair, n2e, n2o, out_grad, w_up, w_down, bufs, n):
    rows, width = n2e.shape
    hidden = w_up.shape[1]
    first = bufs is None
    any_spec = pl.BlockSpec(memory_space=pl.ANY)
    blk = lambda c: pl.BlockSpec((1, rows, c), lambda i, ids: (2 * pair + i, 0, 0))
    buf_shapes = [
        jax.ShapeDtypeStruct((n, rows, hidden), BF16),
        jax.ShapeDtypeStruct((n, rows, hidden), BF16),
        jax.ShapeDtypeStruct((n, rows, width), BF16),
        jax.ShapeDtypeStruct((n, rows, width), BF16),
    ]
    out = pl.pallas_call(
        partial(mlp_kernel, rows, pair, first),
        grid_spec=pltpu.PrefetchScalarGridSpec(
            num_scalar_prefetch=1,
            grid=(2,),
            in_specs=[
                once((rows, width)),
                once((rows, width)),
                pl.BlockSpec((rows, width), lambda i, ids: ((2 * pair + i) ^ ids[0], 0)),
                once((width, hidden)),
                once((hidden, width)),
            ]
            + ([] if first else [any_spec] * 4),
            out_specs=[blk(hidden), blk(hidden), blk(width), blk(width)]
            + [whole((rows, width))] * 4,
        ),
        out_shape=buf_shapes + [jax.ShapeDtypeStruct((rows, width), BF16)] * 4,
        input_output_aliases={} if first else {6: 0, 7: 1, 8: 2, 9: 3},
        compiler_params=params(56),
        cost_estimate=cost(16 * rows * width * hidden, 4 * width * hidden + 20 * rows * width),
        name=f"mlp{pair}",
    )(ids, n2e, n2o, out_grad, w_up, w_down, *(() if first else bufs))
    return out[:4], out[4], out[5], out[6], out[7]


def turn_kernel(n, rows, ids, *refs):
    ta, ya, tb, yb, res, og, gain = refs[:7]
    weights = refs[7 : 7 + n]
    dres_o, dattn_o, gg_o = refs[7 + n : 10 + n]
    dmix_o = refs[10 + n :]
    half = rows // 2
    dn = jnp.concatenate(
        [
            ta[...].astype(F32) + ya[...].astype(F32),
            tb[...].astype(F32) + yb[...].astype(F32),
        ],
        axis=0,
    )
    xhat, inv = normalize(res[...])
    gg_o[...] = jnp.sum(dn * xhat, axis=0, keepdims=True)
    e = dn * gain[...]
    back = (
        e
        - jnp.mean(e, axis=-1, keepdims=True)
        - xhat * jnp.mean(e * xhat, axis=-1, keepdims=True)
    ) * inv
    d_res = og[...].astype(F32) + back
    dres_o[...] = d_res
    t_pos = ids[0] * rows + lax.broadcasted_iota(jnp.int32, (rows, 1), 0)
    live = (t_pos < ids[1] * FRAME).astype(F32)
    d_attn = (live * d_res).astype(BF16)
    dattn_o[...] = d_attn
    for w, o in zip(weights, dmix_o):
        o[...] = dot_nt(d_attn, w[...]).astype(BF16)


def turn(ids, parts, res, out_grad, gain, weights):
    n = len(weights)
    rows, width = res.shape
    cols = weights[0].shape[0]
    half = (rows // 2, width)
    return pl.pallas_call(
        partial(turn_kernel, n, rows),
        grid_spec=pltpu.PrefetchScalarGridSpec(
            num_scalar_prefetch=1,
            grid=(1,),
            in_specs=[once(half)] * 4
            + [
                once((rows, width)),
                pl.BlockSpec((rows, width), lambda i, ids: (ids[0], 0)),
                once((1, width)),
            ]
            + [once((cols, width))] * n,
            out_specs=[whole((rows, width)), whole((rows, width)), whole((1, width))]
            + [whole((rows, cols))] * n,
        ),
        out_shape=[
            jax.ShapeDtypeStruct((rows, width), F32),
            jax.ShapeDtypeStruct((rows, width), BF16),
            jax.ShapeDtypeStruct((1, width), F32),
        ]
        + [jax.ShapeDtypeStruct((rows, cols), BF16)] * n,
        compiler_params=params(56),
        cost_estimate=cost(2 * rows * width * cols * n, 2 * n * cols * width + 20 * rows * width),
        name="turn",
    )(ids, *parts, res, out_grad, gain[None, :], *weights)


def backward_kernel(blk, q_ref, k_ref, v_ref, do_ref, logs, delta, cos, sin, out, dq_acc):
    step = pl.program_id(0)
    cols = k_ref.shape[1]
    heads = cols // HEAD_DIM
    count = q_ref.shape[0] // blk

    @pl.when(step == 0)
    def _():
        dq_acc[...] = jnp.zeros_like(dq_acc)

    def block(i, carry, masked):
        start = pl.multiple_of(i * blk, blk)
        rows = pl.ds(start, blk)
        result = []
        for h in range(heads):
            lanes = slice(h * HEAD_DIM, (h + 1) * HEAD_DIM)
            dk, dv = carry[h]
            q, d_out = q_ref[rows, lanes], do_ref[rows, lanes]
            k, v = k_ref[:, lanes], v_ref[:, lanes]
            s = dot_nt(k, q) * SCALE2
            p = jnp.exp2(s - logs[h : h + 1, rows])
            if masked:
                s_pos = lax.broadcasted_iota(jnp.int32, s.shape, 0)
                t_pos = lax.broadcasted_iota(jnp.int32, s.shape, 1)
                p = jnp.where(s_pos <= t_pos, p, 0.0)
            dp = dot_nt(v, d_out)
            ds = (p * (dp - delta[h : h + 1, rows])).astype(BF16)
            dv = dv + dot_nn(p.astype(BF16), d_out)
            dk = dk + dot_nn(ds, q)
            dq_acc[rows, lanes] = dq_acc[rows, lanes] + dot_tn(ds, k)
            result.append((dk, dv))
        return tuple(result)

    zero = jnp.zeros((blk, HEAD_DIM), F32)
    carry = tuple((zero, zero) for _ in range(heads))
    carry = block(step, carry, True)
    carry = lax.fori_loop(step + 1, count, lambda i, c: block(i, c, False), carry)
    own = pl.ds(pl.multiple_of(step * blk, blk), blk)
    c, s = cos[...], sin[...]
    for h in range(heads):
        dk, dv = carry[h]
        dq = dq_acc[own, h * HEAD_DIM : (h + 1) * HEAD_DIM]
        at = h * HEAD_DIM
        out[:, at : at + HEAD_DIM] = ((dq * c - flip(dq) * s) * SCALE).astype(BF16)
        at += cols
        out[:, at : at + HEAD_DIM] = ((dk * c - flip(dk) * s) * SCALE).astype(BF16)
        at += cols
        out[:, at : at + HEAD_DIM] = dv.astype(BF16)


def prepare_kernel(n, ids, mixed, *refs):
    pieces, do_o, delta_o = refs[:n], refs[n], refs[n + 1]
    step = pl.program_id(0)
    rel = step ^ ids[0]
    heads = do_o.shape[1] // HEAD_DIM
    for r in range(n):

        @pl.when(rel == r)
        def _():
            piece = pieces[r][...]
            do_o[...] = piece
            prod = piece.astype(F32) * mixed[0].astype(F32)
            for h in range(heads):
                part = jnp.transpose(prod[:, h * HEAD_DIM : (h + 1) * HEAD_DIM])
                delta_o[0, h : h + 1, :] = jnp.sum(part, axis=0, keepdims=True)


def attend_back(ids, q, k, v, logs, mixed, pieces, cos, sin):
    length, cols = q.shape
    n = len(pieces)
    rows = length // n
    heads = cols // HEAD_DIM
    blk = 512
    d_out, delta = pl.pallas_call(
        partial(prepare_kernel, n),
        grid_spec=pltpu.PrefetchScalarGridSpec(
            num_scalar_prefetch=1,
            grid=(n,),
            in_specs=[pl.BlockSpec((1, rows, cols), lambda i, ids: (i ^ ids[0], 0, 0))]
            + [whole((rows, cols))] * n,
            out_specs=[
                pl.BlockSpec((rows, cols), lambda i, ids: (i, 0)),
                pl.BlockSpec((1, heads, rows), lambda i, ids: (i, 0, 0)),
            ],
        ),
        out_shape=[
            jax.ShapeDtypeStruct((length, cols), BF16),
            jax.ShapeDtypeStruct((n, heads, rows), F32),
        ],
        compiler_params=params(16),
        cost_estimate=cost(4 * length * cols, 6 * length * cols),
        name="prepare",
    )(ids, mixed, *pieces)
    delta = jnp.transpose(delta, (1, 0, 2)).reshape(heads, length)
    row = lambda c: pl.BlockSpec((blk, c), lambda j: (j, 0))
    return pl.pallas_call(
        partial(backward_kernel, blk),
        grid=(length // blk,),
        in_specs=[
            whole((length, cols)),
            row(cols),
            row(cols),
            whole((length, cols)),
            whole((heads, length)),
            whole((heads, length)),
            row(HEAD_DIM),
            row(HEAD_DIM),
        ],
        out_specs=row(3 * cols),
        out_shape=jax.ShapeDtypeStruct((length, 3 * cols), BF16),
        scratch_shapes=[pltpu.VMEM((length, cols), F32)],
        compiler_params=params(48),
        cost_estimate=cost(6 * length * length * cols, 20 * length * cols, length * length),
        name="attend_back",
    )(q, k, v, d_out, logs, delta, cos, sin)


def back_in_kernel(cols, order, ids, grads, wq, wk, wv, *rest):
    out = rest[-1]
    g = grads[...]
    total = dot_nt(g[:, :cols], wq[...])
    total = total + dot_nt(g[:, cols : 2 * cols], wk[...])
    total = total + dot_nt(g[:, 2 * cols :], wv[...])
    if len(rest) == 2:
        total = total + rest[0][0].astype(F32)
    out[0] = total.astype(BF16)


def back_in(ids, grads, wq, wk, wv, blocks, parity, recv=None):
    length = grads.shape[0]
    width, cols = wq.shape
    rows = length // blocks
    half = blocks // 2
    pick = lambda i, ids: ((2 * (half - 1 - i) + parity) ^ ids[0], 0)
    slot = pl.BlockSpec((1, rows, width), lambda i, ids: (half - 1 - i, 0, 0))
    extra = [] if recv is None else [recv]
    return pl.pallas_call(
        partial(back_in_kernel, cols, None),
        grid_spec=pltpu.PrefetchScalarGridSpec(
            num_scalar_prefetch=1,
            grid=(half,),
            in_specs=[
                pl.BlockSpec((rows, 3 * cols), pick),
                once((width, cols)),
                once((width, cols)),
                once((width, cols)),
            ]
            + [slot] * len(extra),
            out_specs=slot,
        ),
        out_shape=jax.ShapeDtypeStruct((half, rows, width), BF16),
        compiler_params=params(32),
        cost_estimate=cost(3 * length * width * cols, 2 * length * width),
        name=f"back_in{parity}",
    )(ids, grads, wq, wk, wv, *extra)


def finish_kernel(rows, ids, ta, ya, tb, yb, tok, dres, gain, own_o, buf_o, gg_o):
    dn = jnp.concatenate(
        [
            ta[...].astype(F32) + ya[...].astype(F32),
            tb[...].astype(F32) + yb[...].astype(F32),
        ],
        axis=0,
    )
    xhat, inv = normalize(tok[...].astype(F32))
    gg_o[...] = jnp.sum(dn * xhat, axis=0, keepdims=True)
    e = dn * gain[...]
    back = (
        e
        - jnp.mean(e, axis=-1, keepdims=True)
        - xhat * jnp.mean(e * xhat, axis=-1, keepdims=True)
    ) * inv
    grad = (dres[...] + back).astype(BF16)
    own_o[...] = grad
    buf_o[...] = grad


def finish(ids, parts, tokens, d_res, gain):
    rows, width = d_res.shape
    half = (rows // 2, width)
    mine = pl.BlockSpec((rows, width), lambda i, ids: (ids[0], 0))
    return pl.pallas_call(
        partial(finish_kernel, rows),
        grid_spec=pltpu.PrefetchScalarGridSpec(
            num_scalar_prefetch=1,
            grid=(1,),
            in_specs=[once(half)] * 4 + [mine, once((rows, width)), once((1, width))],
            out_specs=[whole((rows, width)), mine, whole((1, width))],
        ),
        out_shape=[
            jax.ShapeDtypeStruct((rows, width), BF16),
            jax.ShapeDtypeStruct(tokens.shape, BF16),
            jax.ShapeDtypeStruct((1, width), F32),
        ],
        compiler_params=params(40),
        cost_estimate=cost(20 * rows * width, 16 * rows * width),
        name="finish",
    )(ids, *parts, tokens, d_res, gain[None, :])


def close_kernel(rows, ids, ta, ya, tb, yb, res, own_o, buf_o):
    total = jnp.concatenate(
        [
            ta[...].astype(F32) + ya[...].astype(F32),
            tb[...].astype(F32) + yb[...].astype(F32),
        ],
        axis=0,
    )
    t_pos = ids[0] * rows + lax.broadcasted_iota(jnp.int32, (rows, 1), 0)
    live = (t_pos < ids[1] * FRAME).astype(F32)
    out = (res[...] + live * total).astype(BF16)
    own_o[...] = out
    buf_o[...] = out


def close(ids, parts, res, length):
    rows, width = res.shape
    half = (rows // 2, width)
    return pl.pallas_call(
        partial(close_kernel, rows),
        grid_spec=pltpu.PrefetchScalarGridSpec(
            num_scalar_prefetch=1,
            grid=(1,),
            in_specs=[once(half)] * 4 + [once((rows, width))],
            out_specs=[
                whole((rows, width)),
                pl.BlockSpec((rows, width), lambda i, ids: (ids[0], 0)),
            ],
        ),
        out_shape=[
            jax.ShapeDtypeStruct((rows, width), BF16),
            jax.ShapeDtypeStruct((length, width), BF16),
        ],
        compiler_params=params(32),
        cost_estimate=cost(4 * rows * width, 12 * rows * width),
        name="close",
    )(ids, *parts, res)


def grad_out_kernel(n, mixed, *refs):
    pieces, out = refs[:n], refs[n]
    total = dot_tn(mixed[0], pieces[0][...])
    for r in range(1, n):
        total = total + dot_tn(mixed[r], pieces[r][...])
    out[...] = total.astype(BF16)


def grad_out_of(mixed, pieces):
    n, rows, cols = mixed.shape
    width = pieces[0].shape[1]
    tile = 512
    return pl.pallas_call(
        partial(grad_out_kernel, n),
        grid=(width // tile,),
        in_specs=[once((n, rows, cols))]
        + [pl.BlockSpec((rows, tile), lambda i: (0, i))] * n,
        out_specs=pl.BlockSpec((cols, tile), lambda i: (0, i)),
        out_shape=jax.ShapeDtypeStruct((cols, width), BF16),
        compiler_params=params(32),
        cost_estimate=cost(2 * n * rows * cols * width, 2 * n * rows * width),
        name="grad_out",
    )(mixed, *pieces)


def swap(value, bit, n):
    return lax.ppermute(value, "head", [(i, i ^ bit) for i in range(n)])


def gather(own, n):
    if n != 8:
        pieces = [own]
        bit = 1
        while bit < n:
            pieces = pieces + [swap(p, bit, n) for p in pieces]
            bit *= 2
        return pieces
    half = own.shape[0] // 2
    p2, p4, p1 = swap(own, 2, n), swap(own, 4, n), swap(own, 1, n)
    p6a, p6b = swap(p4[:half], 2, n), swap(p2[half:], 4, n)
    p3, p5 = swap(p2, 1, n), swap(p4, 1, n)
    p6 = jnp.concatenate([p6a, p6b], axis=0)
    p7 = jnp.concatenate([swap(p6a, 1, n), swap(p6b, 1, n)], axis=0)
    return [own, p1, p2, p3, p4, p5, p6, p7]


def exchange(pieces, n):
    order = sorted(range(1, n), key=lambda r: (-(r & ~1), r))
    got = {0: pieces[0]}
    for r in order:
        got[r] = swap(pieces[r], r, n)
    return [got[r] for r in range(n)]


def add(a, b):
    return (a.astype(F32) + b.astype(F32)).astype(BF16)


def scatter_pairs(chip, n):
    if n != 8:
        live = dict(chip)
        bit = n // 2
        while bit > 2:
            for r in [r for r in live if r < bit]:
                live[r] = add(live[r], swap(live.pop(r | bit), bit, n))
            bit //= 2
        half = live[0].shape[0] // 2
        got = swap(live[2], 2, n)
        return live[0][:half], got[:half], live[0][half:], got[half:]
    half = chip[0].shape[0] // 2
    a6, b6 = swap(chip[6][:half], 2, n), swap(chip[6][half:], 4, n)
    a2, b4 = swap(chip[2][:half], 2, n), swap(chip[4][half:], 4, n)
    ya = swap(add(chip[4][:half], a6), 4, n)
    xb = swap(add(chip[2][half:], b6), 2, n)
    keep_a = chip[0][:half].astype(F32) + a2.astype(F32)
    keep_b = chip[0][half:].astype(F32) + b4.astype(F32)
    return keep_a, ya, keep_b, xb


def assemble(buf, pieces, h, rows):
    for r in range(1, len(pieces)):
        buf = lax.dynamic_update_slice_in_dim(buf, pieces[r], (h ^ r) * rows, 0)
    return buf


def after(value, *others):
    return lax.optimization_barrier((value,) + others)[0]


def clip_sum(grad, dim):
    return lax.psum_scatter(grad, "clip", scatter_dimension=dim, tiled=True).astype(F32)


def local(
    n,
    tokens,
    frame_count,
    norm1_gain,
    w_query,
    w_key,
    w_value,
    w_out,
    norm2_gain,
    w_up,
    w_down,
    out_grad,
):
    length, width = tokens.shape
    rows = length // n
    cols = w_query.shape[1]
    h = lax.axis_index("head").astype(jnp.int32)
    ids = jnp.stack([h, frame_count[0].astype(jnp.int32)])

    out_weights = gather(w_out, n)
    norm1, query, key, value, cos, sin = project(
        tokens, norm1_gain, w_query, w_key, w_value, n
    )
    mixed, logs = attend(ids, query, key, value, n)
    heads = cols // HEAD_DIM
    logs = jnp.transpose(logs, (1, 0, 2)).reshape(heads, length)
    mixed_own = exchange([mixed[r] for r in range(n)], n)
    res, norm2 = merge(ids, mixed_own, out_weights, tokens, norm2_gain)
    norm2_pieces = gather(norm2, n)

    bufs = None
    chip_dn, chip_ml = {}, {}
    mlp_pairs = {}
    for pair in range(n // 2):
        bufs, dne, dno, mle, mlo = mlp(
            ids,
            pair,
            norm2_pieces[2 * pair],
            norm2_pieces[2 * pair + 1],
            out_grad,
            w_up,
            w_down,
            bufs,
            n,
        )
        chip_dn[2 * pair] = add(dne, swap(dno, 1, n))
        mlp_pairs[2 * pair] = (mle, mlo)
    act, d_up, norm2_all, d_mlp = bufs
    dn_parts = scatter_pairs(chip_dn, n)
    turned = turn(ids, dn_parts, res, out_grad, norm2_gain, out_weights)
    d_res, d_attn, gain2 = turned[:3]
    d_mixed = exchange(turned[3:], n)

    flat = lambda a: a.reshape(length, a.shape[-1])
    grad_down = clip_sum(dot_tn(flat(act), flat(d_mlp)).astype(BF16), 1)
    grad_up = clip_sum(dot_tn(flat(norm2_all), flat(d_up)).astype(BF16), 0)

    grads = attend_back(ids, query, key, value, logs, mixed, d_mixed, cos, sin)

    gate = d_mixed[n - 1]
    d_attn_pieces = gather(after(d_attn, gate), n)
    grad_out = clip_sum(grad_out_of(mixed, d_attn_pieces), 1)
    for r, (mle, mlo) in mlp_pairs.items():
        chip_ml[r] = add(mle, swap(after(mlo, gate), 1, n))
    ml_parts = scatter_pairs(chip_ml, n)
    out_own, out_buf = close(ids, ml_parts, res, length)
    output = assemble(out_buf, gather(out_own, n), h, rows)

    odd = back_in(ids, grads, w_query, w_key, w_value, n, 1)
    got = swap(odd, 1, n)
    even = back_in(ids, grads, w_query, w_key, w_value, n, 0, got)
    d1_parts = scatter_pairs({2 * i: even[i] for i in range(n // 2)}, n)
    in_own, in_buf, gain1 = finish(ids, d1_parts, tokens, d_res, norm1_gain)
    in_grad = assemble(in_buf, gather(in_own, n), h, rows)

    grad_qkv = clip_sum(dot_tn(norm1, grads).astype(BF16), 0)
    gains = lax.psum(jnp.concatenate([gain1, gain2], axis=0), ("clip", "head"))
    share = width // lax.axis_size("clip")
    gains = lax.dynamic_slice_in_dim(gains, lax.axis_index("clip") * share, share, 1)
    return (
        output,
        in_grad,
        gains[0],
        grad_qkv[:, :cols],
        grad_qkv[:, cols : 2 * cols],
        grad_qkv[:, 2 * cols :],
        grad_out,
        gains[1],
        grad_up,
        grad_down,
    )


def solution(mesh):
    placed = (
        P("clip", None),
        P("clip"),
        P(),
        P(None, "head"),
        P(None, "head"),
        P(None, "head"),
        P("head", None),
        P(),
        P(None, "head"),
        P("head", None),
        P("clip", None),
    )
    return jax.shard_map(
        partial(local, mesh.shape["head"]),
        mesh=mesh,
        in_specs=placed,
        out_specs=(
            P("clip", None),
            P("clip", None),
            P("clip"),
            P("clip", "head"),
            P("clip", "head"),
            P("clip", "head"),
            P("head", "clip"),
            P("clip"),
            P("clip", "head"),
            P("head", "clip"),
        ),
        check_vma=False,
    )
```
